32 devices in a mesh: box: 32 (over z, y, x, core).
Axes of the slice: x: 2, y: 2, z: 4, core: 2. Of those that a mesh axis runs over, the one named last changes fastest.
Arguments:
- basis_vector: float32 [16, 131072], P(None, 'box'), may hold values from -600 to 600
- diagonal: float32 [131072], P('box'), may hold values from 0.25 to 2
- coords: int32 [2, 131072], P(None, 'box'), may hold values from 0 to 4095
- phase_scale: int32 [1], replicated, may hold values from 1 to 8190
- sketch_rows: int32 [131072], P('box'), may hold values from 0 to 2047
- sketch_signs: int32 [131072], P('box'), may hold values from 0 to 1
Outputs:
- new_basis: float32 [16, 131072], P(None, 'box')
- sketch: float32 [16, 2048], replicated
- arnoldi: float32 [2, 16], replicated
The draws below stay inside these ranges and needn't reach their ends.
All inputs are finite; a program needn't handle non-finite values.
Results may differ from the reference program's by a relative error of at most 0.00019.
Values sent between devices are 32-bit elements; how exact they have to be, the bound alone decides.
A program may use at most 64 MiB of HBM per device.

```python
import math
import jax
import jax.numpy as jnp
from jax import lax

RANK = 16
WIDTH = 32
LEAF = 32
GRID = 4096
SKETCH = 2048
NRHS = 16
BOX_DEV = 128
NPTS = 131072
SECTIONS = 5
N_BOX = 32


def draw_basis_vector(key, part):
    key_scale, key_normal = jax.random.split(key, 2)
    position = jnp.arange(NPTS, dtype=jnp.float32) / NPTS
    row_scale = jnp.exp(jax.random.uniform(key_scale, (NPTS,), jnp.float32, 0.0, math.log(10.0))) * jnp.exp(position * math.log(3.0))
    normal_part = jax.random.normal(key_normal, (NRHS, NPTS), jnp.float32)
    return jnp.clip(normal_part, -4.0, 4.0) * row_scale[None, :]


def with_ends(drawn, own_key, low, largest):
    spot = [jax.random.randint(jax.random.fold_in(own_key, axis), (), 0, length) for axis, length in enumerate(drawn.shape)]
    widest = drawn.shape.index(max(drawn.shape))
    next_to = spot[:widest] + [(spot[widest] + 1) % drawn.shape[widest]] + spot[widest + 1:]
    return drawn.at[tuple(spot)].set(low).at[tuple(next_to)].set(largest)


def levels(own_key, shape, pieces, low, top_value):
    gain, own = 1.0, jax.random.fold_in(own_key, 6)
    for dim, shards_of in pieces:
        steps = jnp.exp(jax.random.uniform(jax.random.fold_in(own, dim), (shards_of,), jnp.float32, low / len(pieces), top_value / len(pieces)))
        gain = gain * jnp.repeat(steps, shape[dim] // shards_of).reshape([-1 if axis == dim else 1 for axis in range(len(shape))])
    return gain


def setup_inputs(seed: int = 0) -> dict:
    keys = jax.random.split(jax.random.key(seed), 7)
    basis_vector = draw_basis_vector(jax.random.fold_in(keys[6], 71), 0)
    diagonal = jnp.clip(jnp.exp(math.log(2.0) - 2.0794415 * jax.random.uniform(keys[1], (NPTS,), jnp.float32) ** levels(keys[1], (NPTS,), ((0, 32),), -0.2, 0.2)), 0.25, 2.0)
    coords = with_ends(jax.random.randint(keys[2], (2, NPTS), 0, GRID), jax.random.fold_in(keys[2], 1), 0, GRID - 1).astype(jnp.int32)
    phase_scale = jax.random.randint(keys[3], (1,), 1, 8191).astype(jnp.int32)
    sketch_rows = with_ends(jax.random.randint(keys[4], (NPTS,), 0, SKETCH), jax.random.fold_in(keys[4], 1), 0, SKETCH - 1).astype(jnp.int32)
    sketch_signs = with_ends(jax.random.randint(keys[5], (NPTS,), 0, 2), jax.random.fold_in(keys[5], 1), 0, 1).astype(jnp.int32)
    return {"basis_vector": basis_vector, "diagonal": diagonal, "coords": coords, "phase_scale": phase_scale, "sketch_rows": sketch_rows, "sketch_signs": sketch_signs}


modulus = 8191
epsilon = 1e-06

def leaf_table(coords, phase_scale):
    scale_mod = phase_scale[0] % modulus
    freq = jnp.arange(RANK, dtype=jnp.int32)
    freq_first = freq % 4 + 1
    freq_second = freq // 4 + 1
    linear = (freq_first[:, None] * coords[0][None, :] + freq_second[:, None] * coords[1][None, :]) % modulus
    phase = scale_mod * linear % modulus
    angle = phase.astype(jnp.float32) * (2.0 * math.pi / modulus)
    return jnp.concatenate([jnp.cos(angle), jnp.sin(angle)], 0) * (1.0 / math.sqrt(LEAF))

def translations(box_ids, segment_num, phase_scale):
    scale_mod = phase_scale[0] % modulus
    base_key = (box_ids * 37 + 101 * segment_num) % (modulus - 1) + 1
    unit_phase = scale_mod * base_key % modulus
    indices = jnp.arange(WIDTH, dtype=jnp.int32)
    prod_a = (indices[:, None] + 1) * (indices[None, :] + 2) % modulus
    prod_b = (indices[:, None] + 3) * (indices[None, :] + 1) % modulus
    phase_a = prod_a[:, :, None] * unit_phase[None, None, :] % modulus
    phase_b = (prod_b[:, :, None] * unit_phase[None, None, :] + 4096) % modulus
    factor = 2.0 * math.pi / modulus
    ident = jnp.eye(WIDTH, dtype=jnp.float32)[:, :, None]
    own_map = 0.85 * ident + 0.35 / math.sqrt(WIDTH) * jnp.cos(phase_a.astype(jnp.float32) * factor)
    cross_map = 0.6 / math.sqrt(WIDTH) * jnp.cos(phase_b.astype(jnp.float32) * factor)
    return (own_map, cross_map)

def reference(basis_vector, diagonal, coords, phase_scale, sketch_rows, sketch_signs):
    highest = lax.Precision.HIGHEST
    columns = basis_vector.shape[0]
    points = basis_vector.shape[1]
    box_count = points // LEAF
    leaf_map = leaf_table(coords, phase_scale)
    leaf_boxes = leaf_map.reshape(WIDTH, box_count, LEAF)
    blocks = basis_vector.reshape(columns, box_count, LEAF)
    coeffs = jnp.einsum('wbs,qbs->wqb', leaf_boxes, blocks, precision=highest)
    coeffs = coeffs.reshape(WIDTH, columns, N_BOX, BOX_DEV)
    box_ids = jnp.arange(box_count, dtype=jnp.int32)
    for segment_num in range(SECTIONS):
        stride = 2 ** segment_num
        grouped = coeffs.reshape(WIDTH, columns, N_BOX // (2 * stride), 2, stride, BOX_DEV)
        partner = grouped[:, :, :, ::-1].reshape(WIDTH, columns, N_BOX, BOX_DEV)
        own_map, cross_map = translations(box_ids, segment_num, phase_scale)
        own_map = own_map.reshape(WIDTH, WIDTH, N_BOX, BOX_DEV)
        cross_map = cross_map.reshape(WIDTH, WIDTH, N_BOX, BOX_DEV)
        coeffs = jnp.einsum('wvdg,vqdg->wqdg', own_map, coeffs, precision=highest) + jnp.einsum('wvdg,vqdg->wqdg', cross_map, partner, precision=highest)
    target_coef = coeffs.reshape(WIDTH, columns, box_count)
    applied = jnp.einsum('wbs,wqb->qbs', leaf_boxes, target_coef, precision=highest).reshape(columns, points)
    image = diagonal[None, :] * basis_vector + applied
    inner_vw = lax.optimization_barrier(jnp.mean(basis_vector * image, axis=1))
    square = lax.optimization_barrier(jnp.mean(basis_vector * basis_vector, axis=1)) + epsilon
    projection = inner_vw / square
    residual = image - projection[:, None] * basis_vector
    spread = jnp.sqrt(lax.optimization_barrier(jnp.mean(residual * residual, axis=1)) + epsilon)
    new_basis = residual / spread[:, None]
    sign_values = (2 * sketch_signs - 1).astype(jnp.float32)
    signed = new_basis * sign_values[None, :]
    sketch = jnp.zeros((columns, SKETCH), jnp.float32).at[:, sketch_rows].add(signed) * math.sqrt(SKETCH / points)
    arnoldi = jnp.stack([projection, spread])
    return (new_basis, sketch, arnoldi)
```

```python
import functools
import math

import jax
import jax.numpy as jnp
import numpy as np
from jax import lax
from jax.experimental import pallas as pl
from jax.experimental.pallas import tpu as pltpu
from jax.sharding import PartitionSpec as P

WIDTH = 32
LEAF = 32
SKETCH = 2048
LANES = 128
HIGH = 8
LOW = SKETCH // HIGH
MODULUS = 8191
EPSILON = 1e-06
MESH = pl.DeviceIdType.MESH
F32 = jnp.float32
BF16 = jnp.bfloat16


def sine_series():
    node = np.cos((np.arange(400) + 0.5) * np.pi / 800)
    basis = np.stack([node ** (2 * i) for i in range(6)], 1)
    exact = np.sin(np.pi * node * 4096 / MODULUS) / node
    return np.linalg.lstsq(basis, exact, rcond=None)[0]


SERIES = sine_series()


def remainder(n):
    return n - jnp.floor(n * (1.0 / MODULUS) + 0.5) * float(MODULUS)


def half_sine(n, gain):
    t = remainder(n) * (1.0 / 4096)
    z = t * t
    total = z * float(SERIES[5] * gain) + float(SERIES[4] * gain)
    for c in SERIES[3::-1]:
        total = total * z + float(c * gain)
    return total * t


def scaled_cos(n, amplitude):
    s = half_sine(n, math.sqrt(2.0 * amplitude))
    return amplitude - s * s


def scaled_sin(n, amplitude):
    return scaled_cos(n - 0.25 * MODULUS, amplitude)


def fold(p):
    return (p & MODULUS) + lax.shift_right_logical(p, 13)


def kernel(devices, stages, total_points, scale_ref, x_ref, nb_ref, sketch_ref, arn_ref,
           pts, leaf, mats, kk, cbuf, part, tbuf, work, onehot, skb, ski,
           a_send, a_recv, b_send, b_recv, sum_send, sum_recv, rs_send, rs_recv, ag_recv, own_chunk,
           a_ss, a_rs, b_ss, b_rs, s_ss, s_rs, r_ss, r_rs, g_ss, g_rs):
    me = lax.axis_index("box")
    columns = nb_ref.shape[0]
    halves = columns // 8
    barrier = pltpu.get_barrier_semaphore()

    @pl.loop(1, devices)
    def _(i):
        pl.semaphore_signal(barrier, inc=1, device_id=(lax.rem(me + i, devices),), device_id_type=MESH)

    lane = lax.broadcasted_iota(jnp.int32, (8, LANES), 1)
    sub = lax.broadcasted_iota(jnp.int32, (8, LANES), 0)
    scale = lax.rem(scale_ref[0], MODULUS)

    rows_in = x_ref.shape[0]
    for i in range(rows_in // 4):
        flipped = x_ref[4 * i:4 * i + 4].reshape(LANES, LANES).T
        tbuf[0] = flipped
        for j in range(4):
            pts[4 * i + j] = jnp.concatenate(
                [tbuf[0, 32 * g:32 * g + 32, 32 * j:32 * j + 32] for g in range(4)], axis=1)

    def exact_phase(row):
        return fold(pts[columns + row].astype(jnp.int32) * scale).astype(F32)

    work[0] = exact_phase(0)
    work[1] = exact_phase(1)
    fx = (sub % 4 + 1).astype(F32)
    fy = (sub // 4 + 1).astype(F32)
    unit = 1.0 / math.sqrt(LEAF)

    @pl.loop(0, LEAF)
    def _(s):
        px = work[0, pl.ds(s, 1), :]
        py = work[1, pl.ds(s, 1), :]
        for tile in range(2):
            n = fx * px + (fy + 2.0 * tile) * py
            leaf[s, 8 * tile:8 * tile + 8] = scaled_cos(n, unit)
            leaf[s, 16 + 8 * tile:24 + 8 * tile] = scaled_sin(n, unit)

    for h in range(halves):
        def gather(s, acc):
            tiles = [leaf[s, 8 * t:8 * t + 8] for t in range(4)]
            out = []
            for q in range(8):
                row = pts[8 * h + q, pl.ds(s, 1), :]
                for t in range(4):
                    out.append(acc[4 * q + t] + tiles[t] * row)
            return tuple(out)

        acc = lax.fori_loop(0, LEAF, gather, tuple(jnp.zeros((8, LANES), F32) for _ in range(32)), unroll=2)
        for q in range(8):
            for t in range(4):
                cbuf[pl.ds((8 * h + q) * 32 + 8 * t, 8), :] = acc[4 * q + t]

    blocks = columns * WIDTH // LANES

    def make_maps(low, bits):
        group = 2 ** bits
        places = LANES // group
        mine = lax.rem(me // 2 ** low, group)
        spot = mine * places + lane % places
        box = 4 * (spot % 32) + spot // 32
        member = me + (lane // places - mine) * 2 ** low
        ident = (member * LANES + box) * 37

        @pl.loop(low, low + bits)
        def _(k):
            x = (ident + 101 * k).astype(F32)
            rest = x - jnp.floor(x * (1.0 / (MODULUS - 1))) * float(MODULUS - 1)
            rest = jnp.where(rest < 0.0, rest + float(MODULUS - 1), rest)
            rest = jnp.where(rest >= float(MODULUS - 1), rest - float(MODULUS - 1), rest)
            key = rest.astype(jnp.int32) + 1
            unit_phase = fold(fold(key * scale)).astype(F32)
            wide = sub.astype(F32)
            for m in range(2):
                amplitude = (0.35 if m == 0 else 0.6) / math.sqrt(WIDTH)
                first, second, offset = (1.0, 2.0, 0.0) if m == 0 else (3.0, 1.0, 4096.0)
                mid = unit_phase * (wide + (8.0 + first))
                far = unit_phase * (wide + (16.0 + first))

                @pl.loop(0, WIDTH, unroll=2)
                def _(v):
                    times = v.astype(F32) + second
                    step = scaled_cos(unit_phase * (8.0 * times), 2.0)
                    one = scaled_cos(mid * times + offset, amplitude)
                    two = scaled_cos(far * times + offset, amplitude)
                    mats[2 * k + m, v, 8:16] = one
                    mats[2 * k + m, v, 16:24] = two
                    mats[2 * k + m, v, 0:8] = step * one - two
                    mats[2 * k + m, v, 24:32] = step * two - one

    def exchange(send, recv, ss, rs, low, bits, action):
        group = 2 ** bits
        mine = lax.rem(me // 2 ** low, group)

        @pl.loop(1, group)
        def _(i):
            other = lax.rem(mine + i, group)
            here = other if action is finish_recv else mine
            copy = pltpu.make_async_remote_copy(
                send.at[other], recv.at[here], ss.at[other], rs.at[here],
                device_id=(me + (other - mine) * 2 ** low,), device_id_type=MESH)
            action(copy)
        return mine

    def pack(send, group):
        places = LANES // group
        for j in range(blocks):
            tbuf[j] = cbuf[LANES * j:LANES * (j + 1), :].T
        for d in range(group):
            for j in range(blocks):
                send[d, places * j:places * (j + 1), :] = tbuf[j, places * d:places * (d + 1), :]

    def unpack(recv, group):
        places = LANES // group
        for j in range(blocks):
            for d in range(group):
                tbuf[j, places * d:places * (d + 1), :] = recv[d, places * j:places * (j + 1), :]
        for j in range(blocks):
            cbuf[LANES * j:LANES * (j + 1), :] = tbuf[j].T

    def sketch_of(values, target, make):
        target[...] = jnp.zeros_like(target)

        @pl.loop(0, LEAF // 4)
        def _(c):
            pieces = []
            for i in range(4):
                s = 4 * c + i
                row = pts[columns + 3, pl.ds(s, 1), :]
                high = jnp.floor(row * (1.0 / LOW))
                if make:
                    low = (row - high * LOW).astype(jnp.int32)
                    ids = lax.broadcasted_iota(jnp.int32, (LOW, LANES), 0)
                    onehot[c, :, LANES * i:LANES * (i + 1)] = jnp.where(ids == low, 1.0, 0.0).astype(BF16)
                sign = 2.0 * pts[columns + 4, pl.ds(s, 1), :] - 1.0
                v = values(s) * sign
                top = v.astype(BF16)
                rest = (v - top.astype(F32)).astype(BF16)
                wide = jnp.broadcast_to(high, (columns, LANES))
                masks = [jnp.where(wide == float(g), 1.0, 0.0).astype(BF16) for g in range(HIGH)]
                pieces.append(jnp.concatenate([top * g for g in masks] + [rest * g for g in masks], axis=0))
            left = jnp.concatenate(pieces, axis=1)
            target[...] += lax.dot_general(left, onehot[c], (((1,), (1,)), ((), ())), preferred_element_type=F32)

    nbt = kk

    def start(copy):
        copy.start()

    def finish_recv(copy):
        copy.wait_recv()

    def finish_send(copy):
        copy.wait_send()

    pl.semaphore_wait(barrier, devices - 1)
    for index, (low, bits) in enumerate(stages):
        group = 2 ** bits
        places = LANES // group
        send, recv, ssem, rsem = a_send.at[index], a_recv.at[index], a_ss.at[index], a_rs.at[index]
        pack(send, group)
        mine = exchange(send, recv, ssem, rsem, low, bits, start)
        recv[mine] = send[mine]
        make_maps(low, bits)
        if index == 0:
            for q in range(columns):
                for s in range(LEAF):
                    nbt[s, q:q + 1, :] = pts[q, s:s + 1, :]
            sketch_of(lambda s: nbt[s], skb, True)
        exchange(send, recv, ssem, rsem, low, bits, finish_recv)
        unpack(recv, group)
        for k in range(low, low + bits):
            span = places * 2 ** (k - low)
            full = cbuf[...]
            wide = lax.broadcasted_iota(jnp.int32, full.shape, 1)
            part[...] = jnp.where((wide // span) % 2 == 0,
                                  pltpu.roll(full, LANES - span, 1), pltpu.roll(full, span, 1))
            for h in range(halves):
                def mix(v, acc):
                    own = [mats[2 * k, v, 8 * t:8 * t + 8] for t in range(4)]
                    cross = [mats[2 * k + 1, v, 8 * t:8 * t + 8] for t in range(4)]
                    out = []
                    for q in range(8):
                        row = cbuf[pl.ds((8 * h + q) * 32 + v, 1), :]
                        other = part[pl.ds((8 * h + q) * 32 + v, 1), :]
                        for t in range(4):
                            out.append(acc[4 * q + t] + own[t] * row + cross[t] * other)
                    return tuple(out)

                init = tuple(0.85 * cbuf[pl.ds((8 * h + q) * 32 + 8 * t, 8), :] for q in range(8) for t in range(4))
                acc = lax.fori_loop(0, WIDTH, mix, init, unroll=2)
                for q in range(8):
                    for t in range(4):
                        cbuf[pl.ds((8 * h + q) * 32 + 8 * t, 8), :] = acc[4 * q + t]
        exchange(send, recv, ssem, rsem, low, bits, finish_send)
        send, recv, ssem, rsem = b_send.at[index], b_recv.at[index], b_ss.at[index], b_rs.at[index]
        pack(send, group)
        mine = exchange(send, recv, ssem, rsem, low, bits, start)
        recv[mine] = send[mine]
        exchange(send, recv, ssem, rsem, low, bits, finish_recv)
        unpack(recv, group)
        exchange(send, recv, ssem, rsem, low, bits, finish_send)

    for c in range(LEAF // 8):
        def spread_out(w, acc):
            coef = [cbuf[pl.ds(8 * h * 32 + w, 8, stride=32), :] for h in range(halves)]
            out = []
            for s in range(8):
                row = leaf[8 * c + s, pl.ds(w, 1), :]
                for h in range(halves):
                    out.append(acc[halves * s + h] + coef[h] * row)
            return tuple(out)

        init = tuple(
            jnp.broadcast_to(pts[columns + 2, 8 * c + s:8 * c + s + 1, :], (8, LANES)) * nbt[8 * c + s, 8 * h:8 * h + 8]
            for s in range(8) for h in range(halves))
        acc = lax.fori_loop(0, WIDTH, spread_out, init, unroll=2)
        for s in range(8):
            for h in range(halves):
                part[(8 * c + s) * columns + 8 * h:(8 * c + s) * columns + 8 * h + 8, :] = acc[halves * s + h]

    inner = jnp.zeros((columns, LANES), F32)
    square, energy = inner, inner
    for s in range(LEAF):
        v, image = nbt[s], part[s * columns:(s + 1) * columns, :]
        inner, square, energy = inner + v * image, square + v * v, energy + image * image
    lane_q = lax.broadcasted_iota(jnp.int32, (columns, LANES), 1)
    row_q = lax.broadcasted_iota(jnp.int32, (columns, LANES), 0)
    packed = jnp.zeros((columns, LANES), F32)
    for i, value in enumerate((inner, square, energy)):
        packed = jnp.where(lane_q == row_q + columns * i, jnp.sum(value, axis=1, keepdims=True), packed)
    sum_send[...] = jnp.sum(packed, axis=0, keepdims=True)

    def to_all(source, recv, ss, rs, action):
        @pl.loop(1, devices)
        def _(i):
            other = lax.rem(me + i, devices)
            here = other if action is finish_recv else me
            action(pltpu.make_async_remote_copy(
                source(other), recv.at[here], ss.at[other], rs.at[here],
                device_id=(other,), device_id_type=MESH))

    to_all(lambda d: sum_send, sum_recv, s_ss, s_rs, start)
    sum_recv[me] = sum_send[...]
    sketch_of(lambda s: part[pl.ds(pl.multiple_of(s * columns, columns), columns), :], ski, False)
    to_all(lambda d: sum_send, sum_recv, s_ss, s_rs, finish_recv)
    totals = jnp.sum(sum_recv[...], axis=0)

    def column(i):
        picked = jnp.where(lane_q == row_q + columns * i, jnp.broadcast_to(totals, (columns, LANES)), 0.0)
        return jnp.broadcast_to(jnp.sum(picked, axis=1, keepdims=True) * (1.0 / total_points), (columns, LANES))

    inner_mean, square_mean, energy_mean = column(0), column(1), column(2)
    projection = inner_mean / (square_mean + EPSILON)
    energy = energy_mean - 2.0 * projection * inner_mean + projection * projection * square_mean
    spread = jnp.sqrt(energy + EPSILON)
    inverse = 1.0 / spread
    arn_ref[0] = projection
    arn_ref[1] = spread

    rows_each = rs_send.shape[1]
    factor = math.sqrt(SKETCH / total_points)
    lowest = HIGH * columns
    part_tiles = LOW // LANES
    for n in range(devices):
        flat = n * rows_each
        tile, row = flat // 8, flat % 8
        strip, side = tile // part_tiles, tile % part_tiles
        top = strip * 8 + row
        q0 = top % columns
        cols = slice(side * LANES, (side + 1) * LANES)
        img = ski[top:top + rows_each, cols] + ski[lowest + top:lowest + top + rows_each, cols]
        bas = skb[top:top + rows_each, cols] + skb[lowest + top:lowest + top + rows_each, cols]
        rs_send[n] = (img - projection[q0:q0 + rows_each] * bas) * (factor * inverse[q0:q0 + rows_each])
    to_all(lambda d: rs_send.at[d], rs_recv, r_ss, r_rs, start)
    rs_recv[me] = rs_send[me]

    for s in range(LEAF):
        pts_rows = (part[s * columns:(s + 1) * columns, :] - projection * nbt[s]) * inverse
        nbt[s] = pts_rows
    for q in range(columns):
        for s in range(LEAF):
            pts[q, s:s + 1, :] = nbt[s, q:q + 1, :]
    for i in range(columns // 4):
        for j in range(4):
            for g in range(4):
                tbuf[0, 32 * g:32 * g + 32, 32 * j:32 * j + 32] = pts[4 * i + j, :, 32 * g:32 * g + 32]
        nb_ref[4 * i:4 * i + 4] = tbuf[0].T.reshape(4, 32, LANES)

    to_all(lambda d: rs_send.at[d], rs_recv, r_ss, r_rs, finish_recv)
    own_chunk[...] = jnp.sum(rs_recv[...], axis=0)
    to_all(lambda d: own_chunk, ag_recv, g_ss, g_rs, start)
    ag_recv[me] = own_chunk[...]
    to_all(lambda d: sum_send, sum_recv, s_ss, s_rs, finish_send)
    to_all(lambda d: rs_send.at[d], rs_recv, r_ss, r_rs, finish_send)
    to_all(lambda d: own_chunk, ag_recv, g_ss, g_rs, finish_recv)
    for n in range(devices):
        flat = n * rows_each
        tile, row = flat // 8, flat % 8
        strip, side = tile // part_tiles, tile % part_tiles
        top = strip * 8 + row
        q0, high = top % columns, top // columns
        begin = high * LOW + side * LANES
        sketch_ref[q0:q0 + rows_each, begin:begin + LANES] = ag_recv[n]
    to_all(lambda d: own_chunk, ag_recv, g_ss, g_rs, finish_send)


def body(basis_vector, diagonal, coords, phase_scale, sketch_rows, sketch_signs):
    columns, local_points = basis_vector.shape
    devices = lax.axis_size("box")
    sections = devices.bit_length() - 1
    count = -(-sections // 5)
    stages, low = [], 0
    for i in range(count):
        bits = (sections - low) // (count - i)
        stages.append((low, bits))
        low += bits
    group = 2 ** max(bits for _, bits in stages)
    group_rows = [columns * WIDTH // LANES * (LANES // 2 ** bits) for _, bits in stages]
    extra = jnp.concatenate([
        coords.astype(F32), diagonal[None, :], sketch_rows.astype(F32)[None, :],
        sketch_signs.astype(F32)[None, :], jnp.zeros((3, local_points), F32)], axis=0)
    stacked = jnp.concatenate([basis_vector, extra], axis=0).reshape(columns + 8, local_points // LANES, LANES)
    rows_each = HIGH * columns * LOW // LANES // devices
    vmem = pl.BlockSpec(memory_space=pltpu.VMEM)
    dma = pltpu.SemaphoreType.DMA
    count_rows = max(group_rows)
    new_basis, sketch, arn = pl.pallas_call(
        functools.partial(kernel, devices, stages, local_points * devices),
        out_shape=(
            jax.ShapeDtypeStruct((columns, local_points // LANES, LANES), F32),
            jax.ShapeDtypeStruct((columns, SKETCH), F32),
            jax.ShapeDtypeStruct((2, columns, LANES), F32)),
        in_specs=[pl.BlockSpec(memory_space=pltpu.SMEM), vmem],
        out_specs=(vmem, vmem, vmem),
        scratch_shapes=[
            pltpu.VMEM((columns + 8, LEAF, LANES), F32),
            pltpu.VMEM((LEAF, WIDTH, LANES), F32),
            pltpu.VMEM((2 * sections, WIDTH, WIDTH, LANES), F32),
            pltpu.VMEM((LEAF, columns, LANES), F32),
            pltpu.VMEM((columns * WIDTH, LANES), F32),
            pltpu.VMEM((columns * WIDTH, LANES), F32),
            pltpu.VMEM((columns * WIDTH // LANES, LANES, LANES), F32),
            pltpu.VMEM((2, LEAF, LANES), F32),
            pltpu.VMEM((LEAF // 4, LOW, 4 * LANES), BF16),
            pltpu.VMEM((2 * HIGH * columns, LOW), F32),
            pltpu.VMEM((2 * HIGH * columns, LOW), F32),
            pltpu.VMEM((count, group, count_rows, LANES), F32),
            pltpu.VMEM((count, group, count_rows, LANES), F32),
            pltpu.VMEM((count, group, count_rows, LANES), F32),
            pltpu.VMEM((count, group, count_rows, LANES), F32),
            pltpu.VMEM((1, LANES), F32),
            pltpu.VMEM((devices, 1, LANES), F32),
            pltpu.VMEM((devices, rows_each, LANES), F32),
            pltpu.VMEM((devices, rows_each, LANES), F32),
            pltpu.VMEM((devices, rows_each, LANES), F32),
            pltpu.VMEM((rows_each, LANES), F32),
            dma((count, group)), dma((count, group)), dma((count, group)), dma((count, group)),
            dma((devices,)), dma((devices,)), dma((devices,)), dma((devices,)), dma((devices,)), dma((devices,)),
        ],
        compiler_params=pltpu.CompilerParams(
            collective_id=0, has_side_effects=True, vmem_limit_bytes=60 * 2**20),
        name="gmres",
    )(phase_scale, stacked)
    return new_basis.reshape(columns, local_points), sketch, arn[:, :, 0]


def solution(mesh):
    placed = (P(None, "box"), P("box"), P(None, "box"), P(), P("box"), P("box"))
    return jax.shard_map(
        body, mesh=mesh, in_specs=placed, out_specs=(P(None, "box"), P(), P()), check_vma=False
    )
```

```python
import functools
import math

import jax
import jax.numpy as jnp
import numpy as np
from jax import lax
from jax.experimental import pallas as pl
from jax.experimental.pallas import tpu as pltpu
from jax.sharding import PartitionSpec as P

WIDTH = 32
LEAF = 32
SKETCH = 2048
LANES = 128
HIGH = 8
LOW = SKETCH // HIGH
MODULUS = 8191
EPSILON = 1e-06
MESH = pl.DeviceIdType.MESH
F32 = jnp.float32
BF16 = jnp.bfloat16


def sine_series():
    node = np.cos((np.arange(400) + 0.5) * np.pi / 800)
    basis = np.stack([node ** (2 * i) for i in range(6)], 1)
    exact = np.sin(np.pi * node * 4096 / MODULUS) / node
    return np.linalg.lstsq(basis, exact, rcond=None)[0]


SERIES = sine_series()


def remainder(n):
    return n - jnp.floor(n * (1.0 / MODULUS) + 0.5) * float(MODULUS)


def half_sine(n, gain):
    t = remainder(n) * (1.0 / 4096)
    z = t * t
    total = z * float(SERIES[5] * gain) + float(SERIES[4] * gain)
    for c in SERIES[3::-1]:
        total = total * z + float(c * gain)
    return total * t


def scaled_cos(n, amplitude):
    s = half_sine(n, math.sqrt(2.0 * amplitude))
    return amplitude - s * s


def scaled_sin(n, amplitude):
    return scaled_cos(n - 0.25 * MODULUS, amplitude)


def fold(p):
    return (p & MODULUS) + lax.shift_right_logical(p, 13)


def kernel(devices, stages, total_points, scale_ref, v_ref, coords_ref, diag_ref, rows_ref, signs_ref,
           nb_ref, sketch_ref, arn_ref, raw, pts, leaf, mats, kk, cbuf, part, tbuf, work, onehot, skb, ski,
           a_send, a_recv, b_send, b_recv, sum_send, sum_recv, rs_send, rs_recv, ag_recv, own_chunk,
           a_ss, a_rs, b_ss, b_rs, s_ss, s_rs, r_ss, r_rs, g_ss, g_rs):
    me = lax.axis_index("box")
    columns = nb_ref.shape[0]
    halves = columns // 8
    barrier = pltpu.get_barrier_semaphore()

    @pl.loop(1, devices)
    def _(i):
        pl.semaphore_signal(barrier, inc=1, device_id=(lax.rem(me + i, devices),), device_id_type=MESH)

    lane = lax.broadcasted_iota(jnp.int32, (8, LANES), 1)
    sub = lax.broadcasted_iota(jnp.int32, (8, LANES), 0)
    scale = lax.rem(scale_ref[0], MODULUS)

    for r in range(LANES // 4):
        here = slice(LANES * r, LANES * (r + 1))
        for h in range(halves):
            raw[pl.ds(256 * h + r, 8, stride=32), :] = v_ref[8 * h:8 * h + 8, here]
        pair = coords_ref[:, here].astype(F32)
        raw[columns * 32 + r:columns * 32 + r + 1, :] = pair[0:1]
        raw[columns * 32 + 32 + r:columns * 32 + 33 + r, :] = pair[1:2]
    raw[(columns + 2) * 32:(columns + 3) * 32, :] = diag_ref[...]
    raw[(columns + 3) * 32:(columns + 4) * 32, :] = rows_ref[...].astype(F32)
    raw[(columns + 4) * 32:(columns + 5) * 32, :] = signs_ref[...].astype(F32)
    raw[(columns + 5) * 32:(columns + 8) * 32, :] = jnp.zeros((96, LANES), F32)
    for i in range((columns + 8) // 4):
        flipped = raw[LANES * i:LANES * (i + 1), :].T
        tbuf[0] = flipped
        for j in range(4):
            pts[4 * i + j] = jnp.concatenate(
                [tbuf[0, 32 * g:32 * g + 32, 32 * j:32 * j + 32] for g in range(4)], axis=1)

    def exact_phase(row):
        return fold(pts[columns + row].astype(jnp.int32) * scale).astype(F32)

    work[0] = exact_phase(0)
    work[1] = exact_phase(1)
    fx = (sub % 4 + 1).astype(F32)
    fy = (sub // 4 + 1).astype(F32)
    unit = 1.0 / math.sqrt(LEAF)

    @pl.loop(0, LEAF)
    def _(s):
        px = work[0, pl.ds(s, 1), :]
        py = work[1, pl.ds(s, 1), :]
        for tile in range(2):
            n = fx * px + (fy + 2.0 * tile) * py
            leaf[s, 8 * tile:8 * tile + 8] = scaled_cos(n, unit)
            leaf[s, 16 + 8 * tile:24 + 8 * tile] = scaled_sin(n, unit)

    def gather_half(h):
        def gather(s, acc):
            tiles = [leaf[s, 8 * t:8 * t + 8] for t in range(4)]
            out = []
            for q in range(8):
                row = pts[8 * h + q, pl.ds(s, 1), :]
                for t in range(4):
                    out.append(acc[4 * q + t] + tiles[t] * row)
            return tuple(out)

        acc = lax.fori_loop(0, LEAF, gather, tuple(jnp.zeros((8, LANES), F32) for _ in range(32)), unroll=2)
        for q in range(8):
            for t in range(4):
                cbuf[pl.ds((8 * h + q) * 32 + 8 * t, 8), :] = acc[4 * q + t]

    blocks = 8 * WIDTH // LANES

    def make_maps(low, bits):
        group = 2 ** bits
        places = LANES // group
        mine = lax.rem(me // 2 ** low, group)
        spot = mine * places + lane % places
        box = 4 * (spot % 32) + spot // 32
        member = me + (lane // places - mine) * 2 ** low
        ident = (member * LANES + box) * 37

        @pl.loop(low, low + bits)
        def _(k):
            x = (ident + 101 * k).astype(F32)
            rest = x - jnp.floor(x * (1.0 / (MODULUS - 1))) * float(MODULUS - 1)
            rest = jnp.where(rest < 0.0, rest + float(MODULUS - 1), rest)
            rest = jnp.where(rest >= float(MODULUS - 1), rest - float(MODULUS - 1), rest)
            key = rest.astype(jnp.int32) + 1
            unit_phase = fold(fold(key * scale)).astype(F32)
            wide = sub.astype(F32)
            for m in range(2):
                amplitude = (0.35 if m == 0 else 0.6) / math.sqrt(WIDTH)
                first, second, offset = (1.0, 2.0, 0.0) if m == 0 else (3.0, 1.0, 4096.0)
                mid = unit_phase * (wide + (8.0 + first))
                far = unit_phase * (wide + (16.0 + first))

                @pl.loop(0, WIDTH, unroll=2)
                def _(v):
                    times = v.astype(F32) + second
                    step = scaled_cos(unit_phase * (8.0 * times), 2.0)
                    one = scaled_cos(mid * times + offset, amplitude)
                    two = scaled_cos(far * times + offset, amplitude)
                    mats[2 * k + m, v, 8:16] = one
                    mats[2 * k + m, v, 16:24] = two
                    mats[2 * k + m, v, 0:8] = step * one - two
                    mats[2 * k + m, v, 24:32] = step * two - one

    def exchange(send, recv, ss, rs, low, bits, action):
        group = 2 ** bits
        mine = lax.rem(me // 2 ** low, group)

        @pl.loop(1, group)
        def _(i):
            other = lax.rem(mine + i, group)
            here = other if action is finish_recv else mine
            copy = pltpu.make_async_remote_copy(
                send.at[other], recv.at[here], ss.at[other], rs.at[here],
                device_id=(me + (other - mine) * 2 ** low,), device_id_type=MESH)
            action(copy)
        return mine

    def pack(send, group, h):
        places = LANES // group
        for j in range(blocks):
            at = LANES * (blocks * h + j)
            tbuf[j] = cbuf[at:at + LANES, :].T
        for d in range(group):
            for j in range(blocks):
                send[d, places * j:places * (j + 1), :] = tbuf[j, places * d:places * (d + 1), :]

    def unpack(recv, group, h):
        places = LANES // group
        for j in range(blocks):
            for d in range(group):
                tbuf[j, places * d:places * (d + 1), :] = recv[d, places * j:places * (j + 1), :]
        for j in range(blocks):
            at = LANES * (blocks * h + j)
            cbuf[at:at + LANES, :] = tbuf[j].T

    def sketch_of(values, target, make):
        target[...] = jnp.zeros_like(target)

        @pl.loop(0, LEAF // 4)
        def _(c):
            pieces = []
            for i in range(4):
                s = 4 * c + i
                row = pts[columns + 3, pl.ds(s, 1), :]
                high = jnp.floor(row * (1.0 / LOW))
                if make:
                    low = (row - high * LOW).astype(jnp.int32)
                    ids = lax.broadcasted_iota(jnp.int32, (LOW, LANES), 0)
                    onehot[c, :, LANES * i:LANES * (i + 1)] = jnp.where(ids == low, 1.0, 0.0).astype(BF16)
                sign = 2.0 * pts[columns + 4, pl.ds(s, 1), :] - 1.0
                v = values(s) * sign
                top = v.astype(BF16)
                rest = (v - top.astype(F32)).astype(BF16)
                wide = jnp.broadcast_to(high, (columns, LANES))
                masks = [jnp.where(wide == float(g), 1.0, 0.0).astype(BF16) for g in range(HIGH)]
                pieces.append(jnp.concatenate([top * g for g in masks] + [rest * g for g in masks], axis=0))
            left = jnp.concatenate(pieces, axis=1)
            target[...] += lax.dot_general(left, onehot[c], (((1,), (1,)), ((), ())), preferred_element_type=F32)

    nbt = kk

    def start(copy):
        copy.start()

    def finish_recv(copy):
        copy.wait_recv()

    def finish_send(copy):
        copy.wait_send()

    for index, (low, bits) in enumerate(stages):
        group = 2 ** bits
        places = LANES // group

        def outward(h, action):
            at = halves * index + h
            return exchange(a_send.at[at], a_recv.at[at], a_ss.at[at], a_rs.at[at], low, bits, action)

        def homeward(h, action):
            at = halves * index + h
            return exchange(b_send.at[at], b_recv.at[at], b_ss.at[at], b_rs.at[at], low, bits, action)

        for h in range(halves):
            at = halves * index + h
            if index == 0:
                gather_half(h)
            pack(a_send.at[at], group, h)
            if index == 0 and h == 0:
                pl.semaphore_wait(barrier, devices - 1)
            mine = outward(h, start)
            a_recv[at, mine] = a_send[at, mine]
        make_maps(low, bits)
        if index == 0:
            for q in range(columns):
                for s in range(LEAF):
                    nbt[s, q:q + 1, :] = pts[q, s:s + 1, :]
            sketch_of(lambda s: nbt[s], skb, True)
        for h in range(halves):
            at = halves * index + h
            outward(h, finish_recv)
            unpack(a_recv.at[at], group, h)
            half = slice(256 * h, 256 * (h + 1))
            for k in range(low, low + bits):
                span = places * 2 ** (k - low)
                full = cbuf[half, :]
                wide = lax.broadcasted_iota(jnp.int32, full.shape, 1)
                part[half, :] = jnp.where((wide // span) % 2 == 0,
                                          pltpu.roll(full, LANES - span, 1), pltpu.roll(full, span, 1))

                def mix(v, acc):
                    own = [mats[2 * k, v, 8 * t:8 * t + 8] for t in range(4)]
                    cross = [mats[2 * k + 1, v, 8 * t:8 * t + 8] for t in range(4)]
                    out = []
                    for q in range(8):
                        row = cbuf[pl.ds((8 * h + q) * 32 + v, 1), :]
                        other = part[pl.ds((8 * h + q) * 32 + v, 1), :]
                        for t in range(4):
                            out.append(acc[4 * q + t] + own[t] * row + cross[t] * other)
                    return tuple(out)

                init = tuple(0.85 * cbuf[pl.ds((8 * h + q) * 32 + 8 * t, 8), :] for q in range(8) for t in range(4))
                acc = lax.fori_loop(0, WIDTH, mix, init, unroll=2)
                for q in range(8):
                    for t in range(4):
                        cbuf[pl.ds((8 * h + q) * 32 + 8 * t, 8), :] = acc[4 * q + t]
            pack(b_send.at[at], group, h)
            mine = homeward(h, start)
            b_recv[at, mine] = b_send[at, mine]
        for h in range(halves):
            outward(h, finish_send)
        for h in range(halves):
            homeward(h, finish_recv)
            unpack(b_recv.at[halves * index + h], group, h)
        for h in range(halves):
            homeward(h, finish_send)

    for c in range(LEAF // 8):
        def spread_out(w, acc):
            coef = [cbuf[pl.ds(8 * h * 32 + w, 8, stride=32), :] for h in range(halves)]
            out = []
            for s in range(8):
                row = leaf[8 * c + s, pl.ds(w, 1), :]
                for h in range(halves):
                    out.append(acc[halves * s + h] + coef[h] * row)
            return tuple(out)

        init = tuple(
            jnp.broadcast_to(pts[columns + 2, 8 * c + s:8 * c + s + 1, :], (8, LANES)) * nbt[8 * c + s, 8 * h:8 * h + 8]
            for s in range(8) for h in range(halves))
        acc = lax.fori_loop(0, WIDTH, spread_out, init, unroll=2)
        for s in range(8):
            for h in range(halves):
                part[(8 * c + s) * columns + 8 * h:(8 * c + s) * columns + 8 * h + 8, :] = acc[halves * s + h]

    inner = jnp.zeros((columns, LANES), F32)
    square, energy = inner, inner
    for s in range(LEAF):
        v, image = nbt[s], part[s * columns:(s + 1) * columns, :]
        inner, square, energy = inner + v * image, square + v * v, energy + image * image
    lane_q = lax.broadcasted_iota(jnp.int32, (columns, LANES), 1)
    row_q = lax.broadcasted_iota(jnp.int32, (columns, LANES), 0)
    packed = jnp.zeros((columns, LANES), F32)
    for i, value in enumerate((inner, square, energy)):
        packed = jnp.where(lane_q == row_q + columns * i, jnp.sum(value, axis=1, keepdims=True), packed)
    sum_send[...] = jnp.sum(packed, axis=0, keepdims=True)

    def to_all(source, recv, ss, rs, action):
        @pl.loop(1, devices)
        def _(i):
            other = lax.rem(me + i, devices)
            here = other if action is finish_recv else me
            action(pltpu.make_async_remote_copy(
                source(other), recv.at[here], ss.at[other], rs.at[here],
                device_id=(other,), device_id_type=MESH))

    to_all(lambda d: sum_send, sum_recv, s_ss, s_rs, start)
    sum_recv[me] = sum_send[...]
    sketch_of(lambda s: part[pl.ds(pl.multiple_of(s * columns, columns), columns), :], ski, False)
    to_all(lambda d: sum_send, sum_recv, s_ss, s_rs, finish_recv)
    totals = jnp.sum(sum_recv[...], axis=0)

    def column(i):
        picked = jnp.where(lane_q == row_q + columns * i, jnp.broadcast_to(totals, (columns, LANES)), 0.0)
        return jnp.broadcast_to(jnp.sum(picked, axis=1, keepdims=True) * (1.0 / total_points), (columns, LANES))

    inner_mean, square_mean, energy_mean = column(0), column(1), column(2)
    projection = inner_mean / (square_mean + EPSILON)
    energy = energy_mean - 2.0 * projection * inner_mean + projection * projection * square_mean
    spread = jnp.sqrt(energy + EPSILON)
    inverse = 1.0 / spread
    for i, value in enumerate((projection, spread)):
        arn_ref[i:i + 1, :] = jnp.sum(jnp.where(lane_q == row_q, value, 0.0), axis=0, keepdims=True)[:, :columns]

    rows_each = rs_send.shape[1]
    factor = math.sqrt(SKETCH / total_points)
    lowest = HIGH * columns
    part_tiles = LOW // LANES
    for n in range(devices):
        flat = n * rows_each
        tile, row = flat // 8, flat % 8
        strip, side = tile // part_tiles, tile % part_tiles
        top = strip * 8 + row
        q0 = top % columns
        cols = slice(side * LANES, (side + 1) * LANES)
        img = ski[top:top + rows_each, cols] + ski[lowest + top:lowest + top + rows_each, cols]
        bas = skb[top:top + rows_each, cols] + skb[lowest + top:lowest + top + rows_each, cols]
        rs_send[n] = (img - projection[q0:q0 + rows_each] * bas) * (factor * inverse[q0:q0 + rows_each])
    to_all(lambda d: rs_send.at[d], rs_recv, r_ss, r_rs, start)
    rs_recv[me] = rs_send[me]

    for s in range(LEAF):
        pts_rows = (part[s * columns:(s + 1) * columns, :] - projection * nbt[s]) * inverse
        nbt[s] = pts_rows
    for q in range(columns):
        for s in range(LEAF):
            pts[q, s:s + 1, :] = nbt[s, q:q + 1, :]
    for i in range(columns // 4):
        for j in range(4):
            for g in range(4):
                tbuf[0, 32 * g:32 * g + 32, 32 * j:32 * j + 32] = pts[4 * i + j, :, 32 * g:32 * g + 32]
        raw[LANES * i:LANES * (i + 1), :] = tbuf[0].T
    for r in range(LANES // 4):
        for h in range(halves):
            nb_ref[8 * h:8 * h + 8, LANES * r:LANES * (r + 1)] = raw[pl.ds(256 * h + r, 8, stride=32), :]

    to_all(lambda d: rs_send.at[d], rs_recv, r_ss, r_rs, finish_recv)
    own_chunk[...] = jnp.sum(rs_recv[...], axis=0)
    to_all(lambda d: own_chunk, ag_recv, g_ss, g_rs, start)
    ag_recv[me] = own_chunk[...]
    to_all(lambda d: sum_send, sum_recv, s_ss, s_rs, finish_send)
    to_all(lambda d: rs_send.at[d], rs_recv, r_ss, r_rs, finish_send)
    to_all(lambda d: own_chunk, ag_recv, g_ss, g_rs, finish_recv)
    for n in range(devices):
        flat = n * rows_each
        tile, row = flat // 8, flat % 8
        strip, side = tile // part_tiles, tile % part_tiles
        top = strip * 8 + row
        q0, high = top % columns, top // columns
        begin = high * LOW + side * LANES
        sketch_ref[q0:q0 + rows_each, begin:begin + LANES] = ag_recv[n]
    to_all(lambda d: own_chunk, ag_recv, g_ss, g_rs, finish_send)


def body(basis_vector, diagonal, coords, phase_scale, sketch_rows, sketch_signs):
    columns, local_points = basis_vector.shape
    devices = lax.axis_size("box")
    sections = devices.bit_length() - 1
    count = -(-sections // 5)
    stages, low = [], 0
    for i in range(count):
        bits = (sections - low) // (count - i)
        stages.append((low, bits))
        low += bits
    group = 2 ** max(bits for _, bits in stages)
    group_rows = [columns * WIDTH // LANES * (LANES // 2 ** bits) for _, bits in stages]
    plane = (local_points // LANES, LANES)
    rows_each = HIGH * columns * LOW // LANES // devices
    vmem = pl.BlockSpec(memory_space=pltpu.VMEM)
    dma = pltpu.SemaphoreType.DMA
    count_rows = max(group_rows)
    halves = columns // 8
    new_basis, sketch, arn = pl.pallas_call(
        functools.partial(kernel, devices, stages, local_points * devices),
        out_shape=(
            jax.ShapeDtypeStruct((columns, local_points), F32),
            jax.ShapeDtypeStruct((columns, SKETCH), F32),
            jax.ShapeDtypeStruct((2, columns), F32)),
        in_specs=[pl.BlockSpec(memory_space=pltpu.SMEM), vmem, vmem, vmem, vmem, vmem],
        out_specs=(vmem, vmem, vmem),
        scratch_shapes=[
            pltpu.VMEM(((columns + 8) * LEAF, LANES), F32),
            pltpu.VMEM((columns + 8, LEAF, LANES), F32),
            pltpu.VMEM((LEAF, WIDTH, LANES), F32),
            pltpu.VMEM((2 * sections, WIDTH, WIDTH, LANES), F32),
            pltpu.VMEM((LEAF, columns, LANES), F32),
            pltpu.VMEM((columns * WIDTH, LANES), F32),
            pltpu.VMEM((columns * WIDTH, LANES), F32),
            pltpu.VMEM((columns * WIDTH // LANES, LANES, LANES), F32),
            pltpu.VMEM((2, LEAF, LANES), F32),
            pltpu.VMEM((LEAF // 4, LOW, 4 * LANES), BF16),
            pltpu.VMEM((2 * HIGH * columns, LOW), F32),
            pltpu.VMEM((2 * HIGH * columns, LOW), F32),
            pltpu.VMEM((count * halves, group, count_rows // halves, LANES), F32),
            pltpu.VMEM((count * halves, group, count_rows // halves, LANES), F32),
            pltpu.VMEM((count * halves, group, count_rows // halves, LANES), F32),
            pltpu.VMEM((count * halves, group, count_rows // halves, LANES), F32),
            pltpu.VMEM((1, LANES), F32),
            pltpu.VMEM((devices, 1, LANES), F32),
            pltpu.VMEM((devices, rows_each, LANES), F32),
            pltpu.VMEM((devices, rows_each, LANES), F32),
            pltpu.VMEM((devices, rows_each, LANES), F32),
            pltpu.VMEM((rows_each, LANES), F32),
            dma((count * halves, group)), dma((count * halves, group)), dma((count * halves, group)), dma((count * halves, group)),
            dma((devices,)), dma((devices,)), dma((devices,)), dma((devices,)), dma((devices,)), dma((devices,)),
        ],
        compiler_params=pltpu.CompilerParams(
            collective_id=0, has_side_effects=True, vmem_limit_bytes=60 * 2**20),
        name="gmres",
    )(phase_scale, basis_vector, coords, diagonal.reshape(plane), sketch_rows.reshape(plane),
      sketch_signs.reshape(plane))
    return new_basis, sketch, arn


def solution(mesh):
    placed = (P(None, "box"), P("box"), P(None, "box"), P(), P("box"), P("box"))
    return jax.shard_map(
        body, mesh=mesh, in_specs=placed, out_specs=(P(None, "box"), P(), P()), check_vma=False
    )
```
